512 devices in a mesh: tm: 16 (over y, z_lo), sx: 8 (over z_hi, core), sy: 4 (over x).
Axes of the slice: x: 4, y: 4, z: 16 (z_hi: 4, z_lo: 4; z = z_hi * 4 + z_lo), core: 2. Of those that a mesh axis runs over, the one named last changes fastest.
Arguments:
- initial: float32 [8, 4, 5, 64, 128], P('sx', 'sy'), may hold values from -6 to 6
- viscosity: float32 [8, 4, 128], P('sx', 'sy'), may hold values from 0.5 to 5
- flux_jacobian: float32 [3, 5, 5], replicated, may hold values from -2 to 2
Outputs:
- nodes: float32 [16, 3, 8, 4, 5, 64, 128], P('tm', None, 'sx', 'sy')
The draws below stay inside these ranges and needn't reach their ends.
All inputs are finite; a program needn't handle non-finite values.
Results may differ from the reference program's by a relative error of at most 0.0001.
Values sent between devices are 32-bit elements; how exact they have to be, the bound alone decides.
A program may use at most 64 MiB of HBM per device.

```python
import math
import jax
import jax.numpy as jnp
from jax import lax

FIELDS = 5
NODES = 64
EZ = 128
ITERS = 2
JF = 3
JC = 2
NTIME = 16
NXE = 8
NYE = 4


def steps_of(stream_key, shape, pieces, smallest, high):
    def one(dim, shards_of):
        heights = jax.random.uniform(jax.random.fold_in(jax.random.fold_in(stream_key, 6), dim), (shards_of,), jnp.float32, smallest / len(pieces), high / len(pieces))
        return jnp.repeat(jnp.exp(heights), shape[dim] // shards_of).reshape((-1,) + (1,) * (len(shape) - dim - 1))

    loudness = one(*pieces[0])
    for cut in pieces[1:]:
        loudness = loudness * one(*cut)
    return loudness


def noise(own_key, extent, scale, bound, pieces=(), kind=jnp.bfloat16):
    loudness = steps_of(own_key, extent, pieces, -0.22, 0.18) if pieces else 1.0
    entries = jax.random.normal(own_key, extent, jnp.float32) * scale * loudness
    return jnp.minimum(jnp.maximum(entries, -bound), bound).astype(kind)


def setup_inputs(seed: int = 0) -> dict:
    arg_keys = jax.random.split(jax.random.key(seed), 4)
    initial = noise(arg_keys[0], (NXE, NYE, FIELDS, NODES, EZ), 1.0, 6.0, ((0, 8), (1, 4)), jnp.float32)
    viscosity = jnp.clip(jnp.exp(math.log(5.0) - 2.3025851 * jax.random.uniform(arg_keys[1], (NXE, NYE, EZ), jnp.float32) ** steps_of(arg_keys[1], (NXE, NYE, EZ), ((0, 8), (1, 4)), -0.2, 0.2)), 0.5, 5.0)
    flux_jacobian = noise(arg_keys[2], (3, FIELDS, FIELDS), 0.35, 2.0, (), jnp.float32)
    return {"initial": initial, "viscosity": viscosity, "flux_jacobian": flux_jacobian}


SIGMA = 3.0
BETA = 0.5
STEP = 0.1
HALF_STEP = 0.05
TWO_THIRDS = 2.0 / 3.0
ONE_THIRD = 1.0 / 3.0
HIGHEST = lax.Precision.HIGHEST
WEIGHTS = ((5.0 / 24.0, 1.0 / 3.0, -1.0 / 24.0), (-1.0 / 24.0, 1.0 / 3.0, 5.0 / 24.0))

def kron_three(first, second, third):
    return jnp.kron(jnp.kron(first, second), third)

def node_tables():
    places = jnp.arange(4)
    row = places[:, None]
    column = places[None, :]
    identity = (row == column).astype(jnp.float32)
    upper = (row + 1 == column).astype(jnp.float32)
    border = identity * ((row == 0) | (row == 3)).astype(jnp.float32)
    line_laplace = 2.0 * identity - upper - upper.T - border
    line_grad = 0.5 * upper - 0.5 * upper.T
    laplace = kron_three(line_laplace, identity, identity) + kron_three(identity, line_laplace, identity) + kron_three(identity, identity, line_laplace) + SIGMA * jnp.eye(64, dtype=jnp.float32)
    grads = jnp.stack([kron_three(line_grad, identity, identity), kron_three(identity, line_grad, identity), kron_three(identity, identity, line_grad)])
    weighting = jnp.where(row == 0, 0.5, math.sqrt(0.5)).astype(jnp.float32)
    cosine = weighting * jnp.cos(math.pi * row.astype(jnp.float32) * (2.0 * column.astype(jnp.float32) + 1.0) / 8.0)
    basis = kron_three(cosine, cosine, cosine)
    line_eigen = 2.0 - 2.0 * jnp.cos(math.pi * places.astype(jnp.float32) / 4.0)
    spectrum = (line_eigen[:, None, None] + line_eigen[None, :, None] + line_eigen[None, None, :]).reshape(64) + SIGMA
    return (laplace, grads, basis, spectrum)

def previous(array, axis):
    widths = [(0, 0)] * array.ndim
    widths[axis] = (1, 0)
    return lax.slice_in_dim(jnp.pad(array, widths), 0, array.shape[axis], axis=axis)

def following(array, axis):
    widths = [(0, 0)] * array.ndim
    widths[axis] = (0, 1)
    return lax.slice_in_dim(jnp.pad(array, widths), 1, array.shape[axis] + 1, axis=axis)

def place(before, after, axis):
    empty = jnp.zeros_like(before)
    return jnp.stack([before, empty, empty, after], axis=axis)

def neighbours(field):
    lattice = field.reshape(field.shape[:4] + (4, 4, 4) + field.shape[-1:])
    along_x = place(previous(lattice[:, :, :, :, 3], 1), following(lattice[:, :, :, :, 0], 1), 4)
    along_y = place(previous(lattice[:, :, :, :, :, 3], 2), following(lattice[:, :, :, :, :, 0], 2), 5)
    along_z = place(previous(lattice[..., 3, :], 6), following(lattice[..., 0, :], 6), 6)
    return (along_x + along_y + along_z).reshape(field.shape)

def apply_operator(field, coeff, flux_jacobian, laplace, grads, coupled):
    volume = jnp.einsum('mn,bxyfnz->bxyfmz', laplace, field, precision=HIGHEST)
    slopes = jnp.einsum('dmn,bxyfnz->dbxyfmz', grads, field, precision=HIGHEST)
    transport = jnp.einsum('dgf,dbxyfmz->bxygmz', flux_jacobian, slopes, precision=HIGHEST)
    return coeff * (volume - BETA * coupled) + transport

def precondition(residue, coeff, basis, spectrum, step):
    inverse = 1.0 / (1.0 + step * coeff * spectrum[:, None])
    modes = jnp.einsum('kn,bxyfnz->bxyfkz', basis, residue, precision=HIGHEST)
    return jnp.einsum('kn,bxyfkz->bxyfnz', basis, modes * inverse, precision=HIGHEST)

def block_jacobi(target, begin, force, step, turns, operate, solve):
    field = begin
    image = -force
    for turn in range(turns):
        if turn > 0:
            image = operate(field)
        field = field + solve(target - field - step * image, step)
    return field

def reference(initial, viscosity, flux_jacobian):
    laplace, grads, basis, spectrum = node_tables()
    coeff = viscosity[None, :, :, None, None, :]

    def operate(field):
        return apply_operator(field, coeff, flux_jacobian, laplace, grads, neighbours(field))

    def solve(residue, step):
        return precondition(residue, coeff, basis, spectrum, step)
    start = initial[None]
    force_zero = -operate(start)
    values = jnp.broadcast_to(initial, (NTIME, 3) + initial.shape)
    forces = jnp.broadcast_to(force_zero[0], (NTIME, 3) + initial.shape)

    def sweep_slice(pair):
        slice_values, slice_forces = pair
        points = [slice_values[m][None] for m in range(3)]
        old = [slice_forces[m][None] for m in range(3)]
        fresh = list(old)
        for node in range(2):
            weight = WEIGHTS[node]
            integral = STEP * (weight[0] * old[0] + weight[1] * old[1] + weight[2] * old[2])
            target = points[node] - HALF_STEP * old[node + 1] + integral
            points[node + 1] = block_jacobi(target, points[node + 1], old[node + 1], HALF_STEP, JF, operate, solve)
            fresh[node + 1] = -operate(points[node + 1])
        return (jnp.concatenate(points, axis=0), jnp.concatenate(fresh, axis=0))

    def pair_forces(pair):
        return -operate(jnp.stack(pair, axis=0))
    for sweep in range(ITERS):
        values, forces = lax.map(sweep_slice, (values, forces))
        correction = STEP * (TWO_THIRDS * forces[:, 1] - ONE_THIRD * forces[:, 0] - ONE_THIRD * forces[:, 2])
        offsets = -STEP * forces[:, 2] + HALF_STEP * (forces[:, 0] + forces[:, 2]) + correction

        def chain_turn(coarse_start, item):
            offset, end_value, end_force = item
            coarse_end = block_jacobi(coarse_start + offset[None], end_value[None], end_force[None], STEP, JC, operate, solve)
            return (coarse_end, (coarse_start[0], coarse_end[0]))
        final_end, (starts, ends) = lax.scan(chain_turn, start, (offsets, values[:, 2], forces[:, 2]))
        if sweep + 1 < ITERS:
            both = lax.map(pair_forces, (starts, ends))
            delta_start = both[:, 0] - forces[:, 0]
            delta_end = both[:, 1] - forces[:, 2]
            forces = jnp.stack([forces[:, 0] + delta_start, forces[:, 1] + 0.5 * (delta_start + delta_end), forces[:, 2] + delta_end], axis=1)
        move_start = starts - values[:, 0]
        move_end = ends - values[:, 2]
        values = jnp.stack([values[:, 0] + move_start, values[:, 1] + 0.5 * (move_start + move_end), values[:, 2] + move_end], axis=1)
    return values
```

```python
import functools
import math

import jax
import jax.numpy as jnp
import ml_dtypes
import numpy as np
from jax import lax
from jax.experimental import pallas as pl
from jax.experimental.pallas import tpu as pltpu
from jax.sharding import PartitionSpec as P

FIELDS, NODES, EZ = 5, 64, 128
WIDE = FIELDS * EZ
NT, NX, NY = 16, 8, 4
DT = 0.1
H1 = 0.05
H2 = 0.1
MESH = pl.DeviceIdType.MESH
F32 = jnp.float32
BF16 = jnp.bfloat16


def tables():
    eye = np.eye(4)
    k = np.arange(4)
    cosine = np.where(k == 0, 0.5, math.sqrt(0.5))[:, None] * np.cos(math.pi * k[:, None] * (2 * k[None, :] + 1) / 8)
    grad = 0.5 * np.eye(4, k=1) - 0.5 * np.eye(4, k=-1)
    slope = cosine @ grad @ cosine.T
    eigen = 2 - 2 * np.cos(math.pi * k / 4)
    spectrum = (eigen[:, None, None] + eigen[None, :, None] + eigen[None, None, :]).reshape(64) + 3.0

    def kron3(a, b, c):
        return np.kron(np.kron(a, b), c)

    low, high = cosine[:, :1].T, cosine[:, 3:].T
    faces_xy = np.concatenate([kron3(low, eye, eye), kron3(high, eye, eye), kron3(eye, low, eye), kron3(eye, high, eye)])
    faces_z = np.concatenate([kron3(eye, eye, low), kron3(eye, eye, high)])
    slopes = np.concatenate([kron3(slope, eye, eye), kron3(eye, slope, eye), kron3(eye, eye, slope)])

    def parts(w):
        w = w.astype(np.float32)
        high_part = w.astype(ml_dtypes.bfloat16)
        low_part = (w - high_part.astype(np.float32)).astype(ml_dtypes.bfloat16)
        return np.concatenate([high_part, high_part, low_part], axis=1)

    basis = kron3(cosine, cosine, cosine).astype(np.float32)
    return (
        parts(faces_xy),
        parts(np.concatenate([slopes, faces_z])),
        parts(faces_xy.T),
        parts(faces_z.T),
        basis,
        np.ascontiguousarray(basis.T),
        np.repeat(spectrum.astype(np.float32)[:, None], EZ, axis=1),
    )


def worker(t, ex, ey):
    return {"tm": ex // 2 * 4 + t % 4, "sx": t // 4 * 2 + ex % 2, "sy": ey}


def wide(x):
    return jnp.concatenate([x] * FIELDS, axis=1)


def split(x):
    high = x.astype(BF16)
    low = (x - high.astype(F32)).astype(BF16)
    return jnp.concatenate([high, low, high], axis=0)


def apply(table, pieces):
    return jnp.dot(table[...], pieces, preferred_element_type=F32)


def exact(table, x):
    return jnp.dot(table[...], x, preferred_element_type=F32, precision=lax.Precision.HIGHEST)


def kernel(initial, viscosity, jac, faces_t, local_t, inject_t, inject_z, basis, basis_t, spectrum, out,
           own, inp, send, recv, st, bs, rh, got,
           in_sem, send_sem, recv_sem, b_send, b_recv, r_send, got_sem, end_send):
    tm, sx, sy = lax.axis_index("tm"), lax.axis_index("sx"), lax.axis_index("sy")
    t = sx // 2 * 4 + tm % 4
    ex = tm // 4 * 2 + sx % 2
    ey = sy
    root = t == 0
    target = {"tm": sx // 2 * 4 + tm // 4, "sx": tm % 4 * 2 + sx % 2, "sy": sy}
    source = {"tm": tm % 4 * 4 + sx // 2, "sx": tm // 4 * 2 + sx % 2, "sy": sy}
    moved = jnp.logical_not(jnp.logical_and(tm // 4 == sx // 2, tm % 4 == sx // 2))
    owner = {"tm": t, "sx": ex, "sy": ey}
    apart = tm // 4 != sx // 2
    around = [
        (worker(t, ex - 1, ey), ex > 0, 0),
        (worker(t, ex + 1, ey), ex < NX - 1, 1),
        (worker(t, ex, ey - 1), ey > 0, 2),
        (worker(t, ex, ey + 1), ey < NY - 1, 3),
    ]
    (D1, D2, CL, HC, U0, U2, M, RM, T0, E1, RU0, RU2, U1N, RU1N, O, G, K0, TMP) = range(18)

    for _, there, side in around:
        @pl.when(jnp.logical_not(there))
        def _(side=side):
            for slot in range(2):
                recv[slot, side] = jnp.zeros((32, WIDE), F32)

    barrier = pltpu.get_barrier_semaphore()

    def greet(device):
        pl.semaphore_signal(barrier, inc=1, device_id=device, device_id_type=MESH)

    for device, there, _ in around:
        @pl.when(there)
        def _(device=device):
            greet(device)

    @pl.when(moved)
    def _():
        greet(source)

    @pl.when(apart)
    def _():
        greet(owner)

    @pl.when(tm > 0)
    def _():
        greet(worker(0, sx, sy))

    @pl.when(tm < NT - 1)
    def _():
        greet({"tm": tm + 1, "sx": sx, "sy": sy})

    @pl.when(root)
    def _():
        def one(k, carry):
            greet(worker(k, ex, ey))
            return carry
        lax.fori_loop(1, NT, one, 0)

    nodal = jnp.concatenate([initial[0, 0, f] for f in range(FIELDS)], axis=1)
    own[0:NODES] = exact(basis, nodal)
    own[NODES:NODES + 8] = wide(jnp.broadcast_to(viscosity[0], (8, EZ)))

    expected = jnp.where(root, NT - 1, 1)
    for there in [there for _, there, _ in around] + [moved, apart, tm > 0]:
        expected = expected + jnp.where(there, 1, 0)
    pl.semaphore_wait(barrier, expected)

    def bring():
        return pltpu.make_async_remote_copy(src_ref=own, dst_ref=inp, send_sem=in_sem.at[0], recv_sem=in_sem.at[1],
                                            device_id=target, device_id_type=MESH)

    @pl.when(moved)
    def _():
        bring().start()
        bring().wait()

    @pl.when(jnp.logical_not(moved))
    def _():
        inp[...] = own[...]

    @pl.when(tm == 0)
    def _():
        got[0] = own[0:NODES]

    c = inp[NODES:NODES + 8, 0:EZ][0:1]
    cl = c * spectrum[...]
    st[CL] = wide(cl)
    st[D1] = wide(1.0 / (1.0 + H1 * cl))
    st[D2] = wide(1.0 / (1.0 + H2 * cl))
    st[HC] = wide(jnp.broadcast_to(0.5 * c, (NODES, EZ)))
    st[U0] = inp[0:NODES]
    st[U2] = inp[0:NODES]
    st[M] = jnp.zeros((NODES, WIDE), F32)
    st[RM] = jnp.zeros((NODES, WIDE), F32)
    lane = lax.broadcasted_iota(jnp.int32, (16, EZ), 1)

    def fields_of(x):
        return [x[:, f * EZ:(f + 1) * EZ] for f in range(FIELDS)]

    def local_part(pieces):
        made = apply(local_t, pieces)
        slopes = [fields_of(made[d * NODES:(d + 1) * NODES]) for d in range(3)]
        transport = []
        for g in range(FIELDS):
            total = None
            for d in range(3):
                for f in range(FIELDS):
                    term = jac[d, g, f] * slopes[d][f]
                    total = term if total is None else total + term
            transport.append(total)
        low = [jnp.where(lane == EZ - 1, 0.0, pltpu.roll(x, EZ - 1, 1)) for x in fields_of(made[192:208])]
        high = [jnp.where(lane == 0, 0.0, pltpu.roll(x, 1, 1)) for x in fields_of(made[208:224])]
        shifted = jnp.concatenate([jnp.concatenate(high, axis=1), jnp.concatenate(low, axis=1)], axis=0)
        return jnp.concatenate(transport, axis=1) - st[HC] * apply(inject_z, split(shifted))

    def couple(values, turn):
        slot = turn % 2
        rows = 16 * len(values)
        pieces = [split(v) for v in values]
        for i, p in enumerate(pieces):
            made = apply(faces_t, p)
            for k in range(4):
                send[k, 16 * i:16 * i + 16] = made[16 * k:16 * k + 16]

        def copy(device, k, side):
            return pltpu.make_async_remote_copy(
                src_ref=send.at[k, pl.ds(0, rows)], dst_ref=recv.at[slot, side, pl.ds(0, rows)],
                send_sem=send_sem.at[k], recv_sem=recv_sem.at[slot, side], device_id=device, device_id_type=MESH)

        for device, there, k in around:
            @pl.when(there)
            def _(device=device, k=k):
                copy(device, k, k ^ 1).start()
        results = [local_part(p) for p in pieces]
        for device, there, k in around:
            @pl.when(there)
            def _(device=device, k=k):
                copy(device, k, k).wait_recv()
        for device, there, k in around:
            @pl.when(there)
            def _(device=device, k=k):
                copy(device, k, k ^ 1).wait_send()
        for i in range(len(values)):
            came = jnp.concatenate([recv[slot, k, 16 * i:16 * i + 16] for k in range(4)], axis=0)
            results[i] = results[i] - st[HC] * apply(inject_t, split(came))
        return results

    def sweep(turn_of):
        st[RU0], st[RU2] = couple([st[U0], st[U2]], turn_of)
        u1 = st[M] + 0.5 * (st[U0] + st[U2])
        ru1 = st[RM] + 0.5 * (st[RU0] + st[RU2])
        k0 = st[CL] * st[U0] + st[RU0]
        k1 = st[CL] * u1 + ru1
        k2 = st[CL] * st[U2] + st[RU2]
        st[K0] = k0
        t0 = st[U0] + H1 * k1 - DT * (5.0 / 24.0 * k0 + 1.0 / 3.0 * k1 - 1.0 / 24.0 * k2)
        st[T0] = t0
        st[E1] = H1 * k2 - DT * (-1.0 / 24.0 * k0 + 1.0 / 3.0 * k1 + 5.0 / 24.0 * k2)
        st[TMP] = st[D1] * (t0 - H1 * ru1)

        def turn(i, carry):
            (rv,) = couple([st[TMP]], turn_of + 1 + i)
            st[TMP] = st[D1] * (st[T0] - H1 * rv)
            return carry
        lax.fori_loop(0, 2, turn, 0)
        u1n = st[TMP]
        st[U1N] = u1n
        t1 = u1n + st[E1]
        st[T0] = t1
        rw, ru1n = couple([st[D1] * (t1 - H1 * st[RU2]), u1n], turn_of + 3)
        st[RU1N] = ru1n
        (rw,) = couple([st[D1] * (st[T0] - H1 * rw)], turn_of + 4)
        u2n = st[D1] * (st[T0] - H1 * rw)
        st[TMP] = u2n
        (ru2n,) = couple([u2n], turn_of + 5)
        u2n = st[TMP]
        k1n = st[CL] * st[U1N] + st[RU1N]
        k2n = st[CL] * u2n + ru2n
        o = -DT * (1.0 / 6.0 * st[K0] + 2.0 / 3.0 * k1n - 5.0 / 6.0 * k2n)
        st[O] = o
        st[G] = st[D2] * (o - H2 * ru2n)
        st[M] = st[U1N] - 0.5 * (st[U0] + u2n)
        st[RM] = st[RU1N] - 0.5 * (st[RU0] + ru2n)

    def iteration(it, carry):
        sweep(it * (7 + t))

        @pl.when(it == 0)
        def _():
            def chain(i, carry):
                s = st[U2] * 1.0
                s = jnp.where(i == 0, st[U0], s)
                st[U0] = s
                (rv,) = couple([st[D2] * s + st[G]], 6 + i)
                st[U2] = st[D2] * (st[U0] + st[O] - H2 * rv)
                return carry
            lax.fori_loop(0, t + 1, chain, 0)
        return carry
    lax.fori_loop(0, 2, iteration, 0)

    def beta_copy():
        return pltpu.make_async_remote_copy(src_ref=st.at[M], dst_ref=got.at[2], send_sem=end_send.at[0],
                                            recv_sem=got_sem.at[2], device_id=owner, device_id_type=MESH)

    @pl.when(apart)
    def _():
        beta_copy().start()

    @pl.when(jnp.logical_not(apart))
    def _():
        got[2] = st[M]

    (rg,) = couple([st[G]], 13 + t)
    bs[0] = st[D2] * (st[O] - H2 * rg)

    def b_copy():
        return pltpu.make_async_remote_copy(src_ref=bs.at[0], dst_ref=bs.at[t], send_sem=b_send.at[0],
                                            recv_sem=b_recv.at[t], device_id=worker(0, ex, ey), device_id_type=MESH)

    @pl.when(jnp.logical_not(root))
    def _():
        b_copy().start()

    def r_copy(k, place):
        return pltpu.make_async_remote_copy(src_ref=rh.at[k], dst_ref=got.at[place], send_sem=r_send.at[k],
                                            recv_sem=got_sem.at[place],
                                            device_id={"tm": jnp.minimum(k + 1, NT - 1), "sx": ex, "sy": ey},
                                            device_id_type=MESH)

    @pl.when(root)
    def _():
        def step(k, carry):
            r = jnp.where(k == 0, inp[0:NODES], rh[jnp.maximum(k - 1, 0)])
            (rv,) = couple([st[D2] * r], 14 + k)
            r = jnp.where(k == 0, inp[0:NODES], rh[jnp.maximum(k - 1, 0)])
            ahead = st[D2] * (r - H2 * rv)

            @pl.when(k > 0)
            def _():
                pltpu.make_async_remote_copy(src_ref=bs.at[0], dst_ref=bs.at[k], send_sem=b_send.at[0],
                                             recv_sem=b_recv.at[k], device_id=worker(k, ex, ey),
                                             device_id_type=MESH).wait_recv()
            rh[k] = ahead + bs[k]

            @pl.when(k < NT - 1)
            def _():
                r_copy(k, 0).start()

            @pl.when(k == NT - 1)
            def _():
                r_copy(k, 1).start()
            return carry
        lax.fori_loop(0, NT, step, 0)

    def emit(node, value):
        for f, x in enumerate(fields_of(value)):
            out[0, node, 0, 0, f] = x

    @pl.when(apart)
    def _():
        beta_copy().wait_recv()

    def hand_on():
        return pltpu.make_async_remote_copy(src_ref=got.at[0], dst_ref=got.at[1], send_sem=end_send.at[1],
                                            recv_sem=got_sem.at[1], device_id={"tm": tm - 1, "sx": sx, "sy": sy},
                                            device_id_type=MESH)

    @pl.when(tm > 0)
    def _():
        r_copy(0, 0).wait_recv()
        hand_on().start()
    first = exact(basis_t, got[0])
    emit(0, first)
    st[TMP] = exact(basis_t, got[2]) + 0.5 * first
    r_copy(0, 1).wait_recv()
    last = exact(basis_t, got[1])
    emit(2, last)
    emit(1, st[TMP] + 0.5 * last)

    @pl.when(apart)
    def _():
        beta_copy().wait_send()

    @pl.when(tm > 0)
    def _():
        hand_on().wait_send()

    @pl.when(jnp.logical_not(root))
    def _():
        b_copy().wait_send()

    @pl.when(root)
    def _():
        def done(k, carry):
            r_copy(k, 0).wait_send()
            return carry
        lax.fori_loop(0, NT, done, 0)


def local(initial, viscosity, flux_jacobian):
    consts = [jnp.asarray(x) for x in tables()]
    vmem = pl.BlockSpec(memory_space=pltpu.VMEM)
    state = (NODES, WIDE)
    return pl.pallas_call(
        kernel,
        out_shape=jax.ShapeDtypeStruct((1, 3, 1, 1, FIELDS, NODES, EZ), F32),
        in_specs=[vmem, vmem, pl.BlockSpec(memory_space=pltpu.SMEM)] + [vmem] * 7,
        out_specs=vmem,
        scratch_shapes=[
            pltpu.VMEM((NODES + 8, WIDE), F32),
            pltpu.VMEM((NODES + 8, WIDE), F32),
            pltpu.VMEM((4, 32, WIDE), F32),
            pltpu.VMEM((2, 4, 32, WIDE), F32),
            pltpu.VMEM((18,) + state, F32),
            pltpu.VMEM((NT,) + state, F32),
            pltpu.VMEM((NT,) + state, F32),
            pltpu.VMEM((3,) + state, F32),
            pltpu.SemaphoreType.DMA((2,)),
            pltpu.SemaphoreType.DMA((4,)),
            pltpu.SemaphoreType.DMA((2, 4)),
            pltpu.SemaphoreType.DMA((1,)),
            pltpu.SemaphoreType.DMA((NT,)),
            pltpu.SemaphoreType.DMA((NT,)),
            pltpu.SemaphoreType.DMA((3,)),
            pltpu.SemaphoreType.DMA((2,)),
        ],
        compiler_params=pltpu.CompilerParams(collective_id=0, has_side_effects=True, vmem_limit_bytes=40 << 20),
    )(initial, viscosity, flux_jacobian, *consts)


def solution(mesh):
    return jax.shard_map(
        local,
        mesh=mesh,
        in_specs=(P("sx", "sy", None, None, None), P("sx", "sy", None), P()),
        out_specs=P("tm", None, "sx", "sy", None, None, None),
        check_vma=False,
    )
```

```python
import functools
import math

import jax
import jax.numpy as jnp
import ml_dtypes
import numpy as np
from jax import lax
from jax.experimental import pallas as pl
from jax.experimental.pallas import tpu as pltpu
from jax.sharding import PartitionSpec as P

FIELDS, NODES, EZ = 5, 64, 128
WIDE = FIELDS * EZ
NT, NX, NY = 16, 8, 4
DT = 0.1
H1 = 0.05
H2 = 0.1
MESH = pl.DeviceIdType.MESH
F32 = jnp.float32
BF16 = jnp.bfloat16


def tables():
    eye = np.eye(4)
    k = np.arange(4)
    cosine = np.where(k == 0, 0.5, math.sqrt(0.5))[:, None] * np.cos(math.pi * k[:, None] * (2 * k[None, :] + 1) / 8)
    grad = 0.5 * np.eye(4, k=1) - 0.5 * np.eye(4, k=-1)
    slope = cosine @ grad @ cosine.T
    eigen = 2 - 2 * np.cos(math.pi * k / 4)
    spectrum = (eigen[:, None, None] + eigen[None, :, None] + eigen[None, None, :]).reshape(64) + 3.0

    def kron3(a, b, c):
        return np.kron(np.kron(a, b), c)

    low, high = cosine[:, :1].T, cosine[:, 3:].T
    faces_xy = np.concatenate([kron3(low, eye, eye), kron3(high, eye, eye), kron3(eye, low, eye), kron3(eye, high, eye)])
    faces_z = np.concatenate([kron3(eye, eye, low), kron3(eye, eye, high)])
    slopes = np.concatenate([kron3(slope, eye, eye), kron3(eye, slope, eye), kron3(eye, eye, slope)])

    def parts(w):
        w = w.astype(np.float32)
        high_part = w.astype(ml_dtypes.bfloat16)
        low_part = (w - high_part.astype(np.float32)).astype(ml_dtypes.bfloat16)
        return np.concatenate([high_part, high_part, low_part], axis=1)

    basis = kron3(cosine, cosine, cosine).astype(np.float32)
    return (
        parts(faces_xy),
        parts(np.concatenate([slopes, faces_z])),
        parts(faces_xy.T),
        parts(faces_z.T),
        basis,
        np.ascontiguousarray(basis.T),
        np.repeat(spectrum.astype(np.float32)[:, None], EZ, axis=1),
    )


def worker(t, ex, ey):
    return {"tm": (ex // 2 + t) % 4 * 4 + t % 4, "sx": t // 4 * 2 + ex % 2, "sy": ey}


def wide(x):
    return jnp.concatenate([x] * FIELDS, axis=1)


def split(x):
    high = x.astype(BF16)
    low = (x - high.astype(F32)).astype(BF16)
    return jnp.concatenate([high, low, high], axis=0)


def apply(table, pieces):
    return jnp.dot(table[...], pieces, preferred_element_type=F32)


def exact(table, x):
    return jnp.dot(table[...], x, preferred_element_type=F32, precision=lax.Precision.HIGHEST)


def kernel(initial_far, viscosity, jac, *refs):
    far, out = refs[:7], refs[7]
    near = refs[8:16]
    initial, faces_t, local_t, inject_t, inject_z, basis, basis_t, spectrum = near
    (own, inp, own_c, inp_c, send, recv, st, bs, rh, got,
     load_sem, in_sem, send_sem, recv_sem, b_send, b_recv, r_send, got_sem, end_send) = refs[16:]
    loads = [pltpu.make_async_copy(a, b, load_sem.at[i]) for i, (a, b) in enumerate(zip((initial_far,) + far, near))]
    for load in loads:
        load.start()
    tm, sx, sy = lax.axis_index("tm"), lax.axis_index("sx"), lax.axis_index("sy")
    t = sx // 2 * 4 + tm % 4
    ex = (tm // 4 + 4 - tm % 4) % 4 * 2 + sx % 2
    ey = sy
    root = t == 0
    kept = (tm // 4 + 4 - sx // 2) % 4
    target = {"tm": tm // 4 * 4 + kept, "sx": (tm % 4 + 4 - kept + sx // 2) % 4 * 2 + sx % 2, "sy": sy}
    source = {"tm": tm // 4 * 4 + (tm % 4 + sx // 2 + 4 - ex // 2) % 4, "sx": ex, "sy": sy}
    moved = ex != sx
    owner = {"tm": t, "sx": ex, "sy": ey}
    maker = worker(tm, sx, sy)
    apart = jnp.logical_not(jnp.logical_and(t == tm, ex == sx))
    around = [
        (worker(t, ex - 1, ey), ex > 0, 0),
        (worker(t, ex + 1, ey), ex < NX - 1, 1),
        (worker(t, ex, ey - 1), ey > 0, 2),
        (worker(t, ex, ey + 1), ey < NY - 1, 3),
    ]
    (D1, D2, CL, HC, U0, U2, M, RM, T0, E1, RU0, RU2, U1N, RU1N, O, G, K0, TMP) = range(18)

    for _, there, side in around:
        @pl.when(jnp.logical_not(there))
        def _(side=side):
            for slot in range(2):
                recv[slot, side] = jnp.zeros((32, WIDE), F32)

    barrier = pltpu.get_barrier_semaphore()

    def greet(device):
        pl.semaphore_signal(barrier, inc=1, device_id=device, device_id_type=MESH)

    for device, there, _ in around:
        @pl.when(there)
        def _(device=device):
            greet(device)

    @pl.when(moved)
    def _():
        greet(source)

    @pl.when(apart)
    def _():
        greet(maker)

    @pl.when(tm > 0)
    def _():
        greet(worker(0, sx, sy))

    @pl.when(tm < NT - 1)
    def _():
        greet({"tm": tm + 1, "sx": sx, "sy": sy})

    @pl.when(root)
    def _():
        def one(k, carry):
            greet(worker(k, ex, ey))
            return carry
        lax.fori_loop(1, NT, one, 0)

    for load in loads:
        load.wait()
    nodal = jnp.concatenate([initial[0, 0, f] for f in range(FIELDS)], axis=1)
    own[...] = exact(basis, nodal)
    own_c[...] = jnp.broadcast_to(viscosity[0], (8, EZ))

    expected = jnp.where(root, NT - 1, 1)
    for there in [there for _, there, _ in around] + [moved, apart, tm > 0]:
        expected = expected + jnp.where(there, 1, 0)
    pl.semaphore_wait(barrier, expected)

    def bring(src, dst, i):
        return pltpu.make_async_remote_copy(src_ref=src, dst_ref=dst, send_sem=in_sem.at[i], recv_sem=in_sem.at[i + 1],
                                            device_id=target, device_id_type=MESH)

    @pl.when(moved)
    def _():
        pair = [bring(own_c, inp_c, 0), bring(own, inp, 2)]
        for one in pair:
            one.start()
        for one in pair:
            one.wait()

    @pl.when(jnp.logical_not(moved))
    def _():
        inp[...] = own[...]
        inp_c[...] = own_c[...]

    @pl.when(tm == 0)
    def _():
        got[0] = own[...]

    c = inp_c[0:1]
    cl = c * spectrum[...]
    st[CL] = wide(cl)
    st[D1] = wide(1.0 / (1.0 + H1 * cl))
    st[D2] = wide(1.0 / (1.0 + H2 * cl))
    st[HC] = wide(jnp.broadcast_to(0.5 * c, (NODES, EZ)))
    st[U0] = inp[...]
    st[U2] = inp[...]
    st[M] = jnp.zeros((NODES, WIDE), F32)
    st[RM] = jnp.zeros((NODES, WIDE), F32)
    lane = lax.broadcasted_iota(jnp.int32, (16, EZ), 1)

    def fields_of(x):
        return [x[:, f * EZ:(f + 1) * EZ] for f in range(FIELDS)]

    def local_part(pieces):
        made = apply(local_t, pieces)
        slopes = [fields_of(made[d * NODES:(d + 1) * NODES]) for d in range(3)]
        transport = []
        for g in range(FIELDS):
            total = None
            for d in range(3):
                for f in range(FIELDS):
                    term = jac[d, g, f] * slopes[d][f]
                    total = term if total is None else total + term
            transport.append(total)
        low = [jnp.where(lane == EZ - 1, 0.0, pltpu.roll(x, EZ - 1, 1)) for x in fields_of(made[192:208])]
        high = [jnp.where(lane == 0, 0.0, pltpu.roll(x, 1, 1)) for x in fields_of(made[208:224])]
        shifted = jnp.concatenate([jnp.concatenate(high, axis=1), jnp.concatenate(low, axis=1)], axis=0)
        return jnp.concatenate(transport, axis=1) - st[HC] * apply(inject_z, split(shifted))

    def couple(values, turn, meanwhile=None):
        slot = turn % 2
        rows = 16 * len(values)
        pieces = [split(v) for v in values]
        for i, p in enumerate(pieces):
            made = apply(faces_t, p)
            for k in range(4):
                send[k, 16 * i:16 * i + 16] = made[16 * k:16 * k + 16]

        def copy(device, k, side):
            return pltpu.make_async_remote_copy(
                src_ref=send.at[k, pl.ds(0, rows)], dst_ref=recv.at[slot, side, pl.ds(0, rows)],
                send_sem=send_sem.at[k], recv_sem=recv_sem.at[slot, side], device_id=device, device_id_type=MESH)

        for device, there, k in around:
            @pl.when(there)
            def _(device=device, k=k):
                copy(device, k, k ^ 1).start()
        if meanwhile is not None:
            meanwhile()
        results = [local_part(p) for p in pieces]
        for device, there, k in around:
            @pl.when(there)
            def _(device=device, k=k):
                copy(device, k, k).wait_recv()
        for device, there, k in around:
            @pl.when(there)
            def _(device=device, k=k):
                copy(device, k, k ^ 1).wait_send()
        for i in range(len(values)):
            came = jnp.concatenate([recv[slot, k, 16 * i:16 * i + 16] for k in range(4)], axis=0)
            results[i] = results[i] - st[HC] * apply(inject_t, split(came))
        return results

    def sweep(turn_of):
        st[RU0], st[RU2] = couple([st[U0], st[U2]], turn_of)
        u1 = st[M] + 0.5 * (st[U0] + st[U2])
        ru1 = st[RM] + 0.5 * (st[RU0] + st[RU2])
        k0 = st[CL] * st[U0] + st[RU0]
        k1 = st[CL] * u1 + ru1
        k2 = st[CL] * st[U2] + st[RU2]
        st[K0] = k0
        t0 = st[U0] + H1 * k1 - DT * (5.0 / 24.0 * k0 + 1.0 / 3.0 * k1 - 1.0 / 24.0 * k2)
        st[T0] = t0
        st[E1] = H1 * k2 - DT * (-1.0 / 24.0 * k0 + 1.0 / 3.0 * k1 + 5.0 / 24.0 * k2)
        st[TMP] = st[D1] * (t0 - H1 * ru1)

        def turn(i, carry):
            (rv,) = couple([st[TMP]], turn_of + 1 + i)
            st[TMP] = st[D1] * (st[T0] - H1 * rv)
            return carry
        lax.fori_loop(0, 2, turn, 0)
        u1n = st[TMP]
        st[U1N] = u1n
        t1 = u1n + st[E1]
        st[T0] = t1
        rw, ru1n = couple([st[D1] * (t1 - H1 * st[RU2]), u1n], turn_of + 3)
        st[RU1N] = ru1n
        (rw,) = couple([st[D1] * (st[T0] - H1 * rw)], turn_of + 4)
        u2n = st[D1] * (st[T0] - H1 * rw)
        st[TMP] = u2n
        (ru2n,) = couple([u2n], turn_of + 5)
        u2n = st[TMP]
        k1n = st[CL] * st[U1N] + st[RU1N]
        k2n = st[CL] * u2n + ru2n
        o = -DT * (1.0 / 6.0 * st[K0] + 2.0 / 3.0 * k1n - 5.0 / 6.0 * k2n)
        st[O] = o
        st[G] = st[D2] * (o - H2 * ru2n)
        st[M] = st[U1N] - 0.5 * (st[U0] + u2n)
        st[RM] = st[RU1N] - 0.5 * (st[RU0] + ru2n)

    def iteration(it, carry):
        sweep(it * (7 + t))

        @pl.when(it == 0)
        def _():
            def chain(i, carry):
                s = st[U2] * 1.0
                s = jnp.where(i == 0, st[U0], s)
                st[U0] = s
                (rv,) = couple([st[D2] * s + st[G]], 6 + i)
                st[U2] = st[D2] * (st[U0] + st[O] - H2 * rv)
                return carry
            lax.fori_loop(0, t + 1, chain, 0)
        return carry
    lax.fori_loop(0, 2, iteration, 0)

    (rg,) = couple([st[G]], 13 + t)
    bs[0] = st[D2] * (st[O] - H2 * rg)

    def b_copy():
        return pltpu.make_async_remote_copy(src_ref=bs.at[0], dst_ref=bs.at[t], send_sem=b_send.at[0],
                                            recv_sem=b_recv.at[t], device_id=worker(0, ex, ey), device_id_type=MESH)

    @pl.when(jnp.logical_not(root))
    def _():
        b_copy().start()

    def beta_copy():
        return pltpu.make_async_remote_copy(src_ref=st.at[M], dst_ref=got.at[2], send_sem=end_send.at[0],
                                            recv_sem=got_sem.at[2], device_id=owner, device_id_type=MESH)

    @pl.when(apart)
    def _():
        beta_copy().start()

    @pl.when(jnp.logical_not(apart))
    def _():
        got[2] = st[M]

    def r_copy(k, place):
        return pltpu.make_async_remote_copy(src_ref=rh.at[k], dst_ref=got.at[place], send_sem=r_send.at[k],
                                            recv_sem=got_sem.at[place],
                                            device_id={"tm": jnp.minimum(k + 1, NT - 1), "sx": ex, "sy": ey},
                                            device_id_type=MESH)

    @pl.when(root)
    def _():
        def step(k, carry):
            r = jnp.where(k == 0, inp[...], rh[jnp.maximum(k - 1, 0)])

            def pass_on():
                @pl.when(k > 0)
                def _():
                    r_copy(k - 1, 0).start()
            (rv,) = couple([st[D2] * r], 14 + k, pass_on)
            r = jnp.where(k == 0, inp[...], rh[jnp.maximum(k - 1, 0)])
            ahead = st[D2] * (r - H2 * rv)

            @pl.when(k > 0)
            def _():
                pltpu.make_async_remote_copy(src_ref=bs.at[0], dst_ref=bs.at[k], send_sem=b_send.at[0],
                                             recv_sem=b_recv.at[k], device_id=worker(k, ex, ey),
                                             device_id_type=MESH).wait_recv()
            rh[k] = ahead + bs[k]

            @pl.when(k == NT - 1)
            def _():
                r_copy(k, 1).start()
            return carry
        lax.fori_loop(0, NT, step, 0)

    def emit(node, value):
        for f, x in enumerate(fields_of(value)):
            out[0, node, 0, 0, f] = x

    @pl.when(apart)
    def _():
        beta_copy().wait_recv()

    def hand_on():
        return pltpu.make_async_remote_copy(src_ref=got.at[0], dst_ref=got.at[1], send_sem=end_send.at[1],
                                            recv_sem=got_sem.at[1], device_id={"tm": tm - 1, "sx": sx, "sy": sy},
                                            device_id_type=MESH)

    @pl.when(tm > 0)
    def _():
        r_copy(0, 0).wait_recv()
        hand_on().start()
    first = exact(basis_t, got[0])
    emit(0, first)
    st[TMP] = exact(basis_t, got[2]) + 0.5 * first
    r_copy(0, 1).wait_recv()
    last = exact(basis_t, got[1])
    emit(2, last)
    emit(1, st[TMP] + 0.5 * last)

    @pl.when(apart)
    def _():
        beta_copy().wait_send()

    @pl.when(tm > 0)
    def _():
        hand_on().wait_send()

    @pl.when(t > 0)
    def _():
        b_copy().wait_send()

    @pl.when(root)
    def _():
        def done(k, carry):
            r_copy(k, 0).wait_send()
            return carry
        lax.fori_loop(0, NT, done, 0)


def local(initial, viscosity, flux_jacobian):
    consts = [jnp.asarray(x) for x in tables()]
    vmem = pl.BlockSpec(memory_space=pltpu.VMEM)
    far = pl.BlockSpec(memory_space=pltpu.HBM)
    state = (NODES, WIDE)
    return pl.pallas_call(
        kernel,
        out_shape=jax.ShapeDtypeStruct((1, 3, 1, 1, FIELDS, NODES, EZ), F32),
        in_specs=[far, vmem, pl.BlockSpec(memory_space=pltpu.SMEM)] + [far] * 7,
        out_specs=vmem,
        scratch_shapes=[pltpu.VMEM(x.shape, x.dtype) for x in [initial] + consts] + [
            pltpu.VMEM(state, F32),
            pltpu.VMEM(state, F32),
            pltpu.VMEM((8, EZ), F32),
            pltpu.VMEM((8, EZ), F32),
            pltpu.VMEM((4, 32, WIDE), F32),
            pltpu.VMEM((2, 4, 32, WIDE), F32),
            pltpu.VMEM((18,) + state, F32),
            pltpu.VMEM((NT,) + state, F32),
            pltpu.VMEM((NT,) + state, F32),
            pltpu.VMEM((3,) + state, F32),
            pltpu.SemaphoreType.DMA((8,)),
            pltpu.SemaphoreType.DMA((4,)),
            pltpu.SemaphoreType.DMA((4,)),
            pltpu.SemaphoreType.DMA((2, 4)),
            pltpu.SemaphoreType.DMA((1,)),
            pltpu.SemaphoreType.DMA((NT,)),
            pltpu.SemaphoreType.DMA((NT,)),
            pltpu.SemaphoreType.DMA((3,)),
            pltpu.SemaphoreType.DMA((2,)),
        ],
        compiler_params=pltpu.CompilerParams(collective_id=0, has_side_effects=True, vmem_limit_bytes=60 << 20),
    )(initial, viscosity, flux_jacobian, *consts)


def solution(mesh):
    return jax.shard_map(
        local,
        mesh=mesh,
        in_specs=(P("sx", "sy", None, None, None), P("sx", "sy", None), P()),
        out_specs=P("tm", None, "sx", "sy", None, None, None),
        check_vma=False,
    )
```

```python
import functools
import math

import jax
import jax.numpy as jnp
import ml_dtypes
import numpy as np
from jax import lax
from jax.experimental import pallas as pl
from jax.experimental.pallas import tpu as pltpu
from jax.sharding import PartitionSpec as P

FIELDS, NODES, EZ = 5, 64, 128
WIDE = FIELDS * EZ
NT, NX, NY = 16, 8, 4
DT = 0.1
H1 = 0.05
H2 = 0.1
MESH = pl.DeviceIdType.MESH
F32 = jnp.float32
BF16 = jnp.bfloat16


def tables():
    eye = np.eye(4)
    k = np.arange(4)
    cosine = np.where(k == 0, 0.5, math.sqrt(0.5))[:, None] * np.cos(math.pi * k[:, None] * (2 * k[None, :] + 1) / 8)
    grad = 0.5 * np.eye(4, k=1) - 0.5 * np.eye(4, k=-1)
    slope = cosine @ grad @ cosine.T
    eigen = 2 - 2 * np.cos(math.pi * k / 4)
    spectrum = (eigen[:, None, None] + eigen[None, :, None] + eigen[None, None, :]).reshape(64) + 3.0

    def kron3(a, b, c):
        return np.kron(np.kron(a, b), c)

    low, high = cosine[:, :1].T, cosine[:, 3:].T
    faces_xy = np.concatenate([kron3(low, eye, eye), kron3(high, eye, eye), kron3(eye, low, eye), kron3(eye, high, eye)])
    faces_z = np.concatenate([kron3(eye, eye, low), kron3(eye, eye, high)])
    slopes = np.concatenate([kron3(slope, eye, eye), kron3(eye, slope, eye), kron3(eye, eye, slope)])

    def parts(w):
        w = w.astype(np.float32)
        high_part = w.astype(ml_dtypes.bfloat16)
        low_part = (w - high_part.astype(np.float32)).astype(ml_dtypes.bfloat16)
        return np.concatenate([high_part, high_part, low_part], axis=1)

    basis = kron3(cosine, cosine, cosine).astype(np.float32)
    return (
        parts(faces_xy),
        parts(np.concatenate([slopes, faces_z])),
        parts(faces_xy.T),
        parts(faces_z.T),
        basis,
        np.ascontiguousarray(basis.T),
        np.repeat(spectrum.astype(np.float32)[:, None], EZ, axis=1),
    )


def worker(t, ex, ey):
    return {"tm": (ex // 2 + t) % 4 * 4 + t % 4, "sx": t // 4 * 2 + ex % 2, "sy": ey}


def wide(x):
    return jnp.concatenate([x] * FIELDS, axis=1)


def split(x):
    high = x.astype(BF16)
    low = (x - high.astype(F32)).astype(BF16)
    return jnp.concatenate([high, low, high], axis=0)


def apply(table, pieces):
    return jnp.dot(table[...], pieces, preferred_element_type=F32)


def exact(table, x):
    return jnp.dot(table[...], x, preferred_element_type=F32, precision=lax.Precision.HIGHEST)


def kernel(initial_far, viscosity, jac, *refs):
    far, out = refs[:7], refs[7]
    near = refs[8:16]
    initial, faces_t, local_t, inject_t, inject_z, basis, basis_t, spectrum = near
    (own, inp, own_c, inp_c, send, recv, st, bs, rh, got,
     load_sem, in_sem, send_sem, recv_sem, b_send, b_recv, r_send, got_sem, end_send) = refs[16:]
    loads = [pltpu.make_async_copy(a, b, load_sem.at[i]) for i, (a, b) in enumerate(zip((initial_far,) + far, near))]
    for load in loads:
        load.start()
    tm, sx, sy = lax.axis_index("tm"), lax.axis_index("sx"), lax.axis_index("sy")
    t = sx // 2 * 4 + tm % 4
    ex = (tm // 4 + 4 - tm % 4) % 4 * 2 + sx % 2
    ey = sy
    root = t == 0
    kept = (tm // 4 + 4 - sx // 2) % 4
    target = {"tm": tm // 4 * 4 + kept, "sx": (tm % 4 + 4 - kept + sx // 2) % 4 * 2 + sx % 2, "sy": sy}
    source = {"tm": tm // 4 * 4 + (tm % 4 + sx // 2 + 4 - ex // 2) % 4, "sx": ex, "sy": sy}
    moved = ex != sx
    owner = {"tm": t, "sx": ex, "sy": ey}
    maker = worker(tm, sx, sy)
    apart = jnp.logical_not(jnp.logical_and(t == tm, ex == sx))
    around = [
        (worker(t, ex - 1, ey), ex > 0, 0),
        (worker(t, ex + 1, ey), ex < NX - 1, 1),
        (worker(t, ex, ey - 1), ey > 0, 2),
        (worker(t, ex, ey + 1), ey < NY - 1, 3),
    ]
    (D1, D2, CL, HC, U0, U2, M, RM, T0, E1, RU0, RU2, U1N, RU1N, O, G, K0, TMP, W2) = range(19)

    for _, there, side in around:
        @pl.when(jnp.logical_not(there))
        def _(side=side):
            for slot in range(2):
                recv[slot, side] = jnp.zeros((32, WIDE), F32)

    barrier = pltpu.get_barrier_semaphore()

    def greet(device):
        pl.semaphore_signal(barrier, inc=1, device_id=device, device_id_type=MESH)

    for device, there, _ in around:
        @pl.when(there)
        def _(device=device):
            greet(device)

    @pl.when(moved)
    def _():
        greet(source)

    @pl.when(apart)
    def _():
        greet(maker)

    @pl.when(tm > 0)
    def _():
        greet(worker(0, sx, sy))

    @pl.when(tm < NT - 1)
    def _():
        greet({"tm": tm + 1, "sx": sx, "sy": sy})

    @pl.when(root)
    def _():
        def one(k, carry):
            greet(worker(k, ex, ey))
            return carry
        lax.fori_loop(1, NT, one, 0)

    for load in loads:
        load.wait()
    nodal = jnp.concatenate([initial[0, 0, f] for f in range(FIELDS)], axis=1)
    own[...] = exact(basis, nodal)
    own_c[...] = jnp.broadcast_to(viscosity[0], (8, EZ))

    expected = jnp.where(root, NT - 1, 1)
    for there in [there for _, there, _ in around] + [moved, apart, tm > 0]:
        expected = expected + jnp.where(there, 1, 0)
    pl.semaphore_wait(barrier, expected)

    def bring(src, dst, i):
        return pltpu.make_async_remote_copy(src_ref=src, dst_ref=dst, send_sem=in_sem.at[i], recv_sem=in_sem.at[i + 1],
                                            device_id=target, device_id_type=MESH)

    @pl.when(moved)
    def _():
        pair = [bring(own_c, inp_c, 0), bring(own, inp, 2)]
        for one in pair:
            one.start()
        for one in pair:
            one.wait()

    @pl.when(jnp.logical_not(moved))
    def _():
        inp[...] = own[...]
        inp_c[...] = own_c[...]

    @pl.when(tm == 0)
    def _():
        got[0] = own[...]

    c = inp_c[0:1]
    cl = c * spectrum[...]
    st[CL] = wide(cl)
    st[D1] = wide(1.0 / (1.0 + H1 * cl))
    st[D2] = wide(1.0 / (1.0 + H2 * cl))
    st[HC] = wide(jnp.broadcast_to(0.5 * c, (NODES, EZ)))
    st[W2] = H2 * st[D2] * st[HC]
    st[U0] = inp[...]
    st[U2] = inp[...]
    st[M] = jnp.zeros((NODES, WIDE), F32)
    st[RM] = jnp.zeros((NODES, WIDE), F32)
    lane = lax.broadcasted_iota(jnp.int32, (16, EZ), 1)

    def fields_of(x):
        return [x[:, f * EZ:(f + 1) * EZ] for f in range(FIELDS)]

    def local_part(pieces):
        made = apply(local_t, pieces)
        slopes = [fields_of(made[d * NODES:(d + 1) * NODES]) for d in range(3)]
        transport = []
        for g in range(FIELDS):
            total = None
            for d in range(3):
                for f in range(FIELDS):
                    term = jac[d, g, f] * slopes[d][f]
                    total = term if total is None else total + term
            transport.append(total)
        low = [jnp.where(lane == EZ - 1, 0.0, pltpu.roll(x, EZ - 1, 1)) for x in fields_of(made[192:208])]
        high = [jnp.where(lane == 0, 0.0, pltpu.roll(x, 1, 1)) for x in fields_of(made[208:224])]
        shifted = jnp.concatenate([jnp.concatenate(high, axis=1), jnp.concatenate(low, axis=1)], axis=0)
        return jnp.concatenate(transport, axis=1) - st[HC] * apply(inject_z, split(shifted))

    def couple(values, turn, meanwhile=None, fold=None):
        slot = turn % 2
        rows = 16 * len(values)
        pieces = [split(v) for v in values]
        for i, p in enumerate(pieces):
            made = apply(faces_t, p)
            for k in range(4):
                send[k, 16 * i:16 * i + 16] = made[16 * k:16 * k + 16]

        def copy(device, k, side):
            return pltpu.make_async_remote_copy(
                src_ref=send.at[k, pl.ds(0, rows)], dst_ref=recv.at[slot, side, pl.ds(0, rows)],
                send_sem=send_sem.at[k], recv_sem=recv_sem.at[slot, side], device_id=device, device_id_type=MESH)

        for device, there, k in around:
            @pl.when(there)
            def _(device=device, k=k):
                copy(device, k, k ^ 1).start()
        if meanwhile is not None:
            meanwhile()
        results = [local_part(p) for p in pieces]
        if fold is not None:
            st[TMP] = fold(results[0])
        for device, there, k in around:
            @pl.when(there)
            def _(device=device, k=k):
                copy(device, k, k).wait_recv()
        for device, there, k in around:
            @pl.when(there)
            def _(device=device, k=k):
                copy(device, k, k ^ 1).wait_send()
        for i in range(len(values)):
            came = jnp.concatenate([recv[slot, k, 16 * i:16 * i + 16] for k in range(4)], axis=0)
            gained = apply(inject_t, split(came))
            results[i] = results[i] - st[HC] * gained if fold is None else st[TMP] + st[W2] * gained
        return results

    def sweep(turn_of):
        st[RU0], st[RU2] = couple([st[U0], st[U2]], turn_of)
        u1 = st[M] + 0.5 * (st[U0] + st[U2])
        ru1 = st[RM] + 0.5 * (st[RU0] + st[RU2])
        k0 = st[CL] * st[U0] + st[RU0]
        k1 = st[CL] * u1 + ru1
        k2 = st[CL] * st[U2] + st[RU2]
        st[K0] = k0
        t0 = st[U0] + H1 * k1 - DT * (5.0 / 24.0 * k0 + 1.0 / 3.0 * k1 - 1.0 / 24.0 * k2)
        st[T0] = t0
        st[E1] = H1 * k2 - DT * (-1.0 / 24.0 * k0 + 1.0 / 3.0 * k1 + 5.0 / 24.0 * k2)
        st[TMP] = st[D1] * (t0 - H1 * ru1)

        def turn(i, carry):
            (rv,) = couple([st[TMP]], turn_of + 1 + i)
            st[TMP] = st[D1] * (st[T0] - H1 * rv)
            return carry
        lax.fori_loop(0, 2, turn, 0)
        u1n = st[TMP]
        st[U1N] = u1n
        t1 = u1n + st[E1]
        st[T0] = t1
        rw, ru1n = couple([st[D1] * (t1 - H1 * st[RU2]), u1n], turn_of + 3)
        st[RU1N] = ru1n
        (rw,) = couple([st[D1] * (st[T0] - H1 * rw)], turn_of + 4)
        u2n = st[D1] * (st[T0] - H1 * rw)
        st[TMP] = u2n
        (ru2n,) = couple([u2n], turn_of + 5)
        u2n = st[TMP]
        k1n = st[CL] * st[U1N] + st[RU1N]
        k2n = st[CL] * u2n + ru2n
        o = -DT * (1.0 / 6.0 * st[K0] + 2.0 / 3.0 * k1n - 5.0 / 6.0 * k2n)
        st[O] = o
        st[G] = st[D2] * (o - H2 * ru2n)
        st[M] = st[U1N] - 0.5 * (st[U0] + u2n)
        st[RM] = st[RU1N] - 0.5 * (st[RU0] + ru2n)

    def iteration(it, carry):
        sweep(it * (7 + t))

        @pl.when(it == 0)
        def _():
            def chain(i, carry):
                s = st[U2] * 1.0
                s = jnp.where(i == 0, st[U0], s)
                st[U0] = s
                (st[U2],) = couple([st[D2] * s + st[G]], 6 + i, None, lambda x: st[D2] * (st[U0] + st[O] - H2 * x))
                return carry
            lax.fori_loop(0, t + 1, chain, 0)
        return carry
    lax.fori_loop(0, 2, iteration, 0)

    (rg,) = couple([st[G]], 13 + t)
    bs[0] = st[D2] * (st[O] - H2 * rg)

    def b_copy():
        return pltpu.make_async_remote_copy(src_ref=bs.at[0], dst_ref=bs.at[t], send_sem=b_send.at[0],
                                            recv_sem=b_recv.at[t], device_id=worker(0, ex, ey), device_id_type=MESH)

    @pl.when(jnp.logical_not(root))
    def _():
        b_copy().start()

    def beta_copy():
        return pltpu.make_async_remote_copy(src_ref=st.at[M], dst_ref=got.at[2], send_sem=end_send.at[0],
                                            recv_sem=got_sem.at[2], device_id=owner, device_id_type=MESH)

    @pl.when(apart)
    def _():
        beta_copy().start()

    @pl.when(jnp.logical_not(apart))
    def _():
        got[2] = st[M]

    def r_copy(k, place):
        return pltpu.make_async_remote_copy(src_ref=rh.at[k], dst_ref=got.at[place], send_sem=r_send.at[k],
                                            recv_sem=got_sem.at[place],
                                            device_id={"tm": jnp.minimum(k + 1, NT - 1), "sx": ex, "sy": ey},
                                            device_id_type=MESH)

    @pl.when(root)
    def _():
        def step(k, carry):
            r = jnp.where(k == 0, inp[...], rh[jnp.maximum(k - 1, 0)])

            def pass_on():
                @pl.when(k > 0)
                def _():
                    r_copy(k - 1, 0).start()
            (ahead,) = couple([st[D2] * r], 14 + k, pass_on, lambda x: st[D2] * (r - H2 * x))

            @pl.when(k > 0)
            def _():
                pltpu.make_async_remote_copy(src_ref=bs.at[0], dst_ref=bs.at[k], send_sem=b_send.at[0],
                                             recv_sem=b_recv.at[k], device_id=worker(k, ex, ey),
                                             device_id_type=MESH).wait_recv()
            rh[k] = ahead + bs[k]

            @pl.when(k == NT - 1)
            def _():
                r_copy(k, 1).start()
            return carry
        lax.fori_loop(0, NT, step, 0)

    def emit(node, value):
        for f, x in enumerate(fields_of(value)):
            out[0, node, 0, 0, f] = x

    @pl.when(apart)
    def _():
        beta_copy().wait_recv()

    def hand_on():
        return pltpu.make_async_remote_copy(src_ref=got.at[0], dst_ref=got.at[1], send_sem=end_send.at[1],
                                            recv_sem=got_sem.at[1], device_id={"tm": tm - 1, "sx": sx, "sy": sy},
                                            device_id_type=MESH)

    @pl.when(tm > 0)
    def _():
        r_copy(0, 0).wait_recv()
        hand_on().start()
    first = exact(basis_t, got[0])
    emit(0, first)
    st[TMP] = exact(basis_t, got[2]) + 0.5 * first
    r_copy(0, 1).wait_recv()
    last = exact(basis_t, got[1])
    emit(2, last)
    emit(1, st[TMP] + 0.5 * last)

    @pl.when(apart)
    def _():
        beta_copy().wait_send()

    @pl.when(tm > 0)
    def _():
        hand_on().wait_send()

    @pl.when(t > 0)
    def _():
        b_copy().wait_send()

    @pl.when(root)
    def _():
        def done(k, carry):
            r_copy(k, 0).wait_send()
            return carry
        lax.fori_loop(0, NT, done, 0)


def local(initial, viscosity, flux_jacobian):
    consts = [jnp.asarray(x) for x in tables()]
    vmem = pl.BlockSpec(memory_space=pltpu.VMEM)
    far = pl.BlockSpec(memory_space=pltpu.HBM)
    state = (NODES, WIDE)
    return pl.pallas_call(
        kernel,
        out_shape=jax.ShapeDtypeStruct((1, 3, 1, 1, FIELDS, NODES, EZ), F32),
        in_specs=[far, vmem, pl.BlockSpec(memory_space=pltpu.SMEM)] + [far] * 7,
        out_specs=vmem,
        scratch_shapes=[pltpu.VMEM(x.shape, x.dtype) for x in [initial] + consts] + [
            pltpu.VMEM(state, F32),
            pltpu.VMEM(state, F32),
            pltpu.VMEM((8, EZ), F32),
            pltpu.VMEM((8, EZ), F32),
            pltpu.VMEM((4, 32, WIDE), F32),
            pltpu.VMEM((2, 4, 32, WIDE), F32),
            pltpu.VMEM((19,) + state, F32),
            pltpu.VMEM((NT,) + state, F32),
            pltpu.VMEM((NT,) + state, F32),
            pltpu.VMEM((3,) + state, F32),
            pltpu.SemaphoreType.DMA((8,)),
            pltpu.SemaphoreType.DMA((4,)),
            pltpu.SemaphoreType.DMA((4,)),
            pltpu.SemaphoreType.DMA((2, 4)),
            pltpu.SemaphoreType.DMA((1,)),
            pltpu.SemaphoreType.DMA((NT,)),
            pltpu.SemaphoreType.DMA((NT,)),
            pltpu.SemaphoreType.DMA((3,)),
            pltpu.SemaphoreType.DMA((2,)),
        ],
        compiler_params=pltpu.CompilerParams(collective_id=0, has_side_effects=True, vmem_limit_bytes=60 << 20),
    )(initial, viscosity, flux_jacobian, *consts)


def solution(mesh):
    return jax.shard_map(
        local,
        mesh=mesh,
        in_specs=(P("sx", "sy", None, None, None), P("sx", "sy", None), P()),
        out_specs=P("tm", None, "sx", "sy", None, None, None),
        check_vma=False,
    )
```
